32 devices in a mesh: dp: 8 (over z, core), expert: 4 (over y, x).
Axes of the slice: x: 2, y: 2, z: 4, core: 2. Of those that a mesh axis runs over, the one named last changes fastest.
Arguments:
- history: bfloat16 [64, 1024, 2048], P(('dp', 'expert')), may hold values from -6 to 6
- lengths: int32 [64], P(('dp', 'expert')), may hold values from 64 to 1024, as said below
- user_query: bfloat16 [64, 2048], P(('dp', 'expert')), may hold values from -1000 to 1000
- pos_item: bfloat16 [64, 2048], P(('dp', 'expert')), may hold values from -6 to 6
- neg_index: int32 [64, 63], P(('dp', 'expert')), may hold values from 0 to 63
- routes: int32 [4096, 2], P(('dp', 'expert')), may hold values from 0 to 3, all different within a row; in each aligned block of 128 rows (0 to 127, 128 to 255, ...) at most 128 rows name the same one
- w_router: bfloat16 [2048, 4], replicated, may hold values from -0.125 to 0.125
- w_gate: bfloat16 [4, 2048, 768], P('expert', 'dp'), may hold values from -0.125 to 0.125
- w_up: bfloat16 [4, 2048, 768], P('expert', 'dp'), may hold values from -0.125 to 0.125
- w_down: bfloat16 [4, 768, 2048], P('expert', None, 'dp'), may hold values from -0.21875 to 0.21875
- out_gain: float32 [2048], replicated, may hold values from 0.25 to 1.75
Outputs:
- losses: float32 [64], P(('dp', 'expert'))
- grad_gate: float32 [4, 2048, 768], P('expert', 'dp')
- grad_up: float32 [4, 2048, 768], P('expert', 'dp')
- grad_down: float32 [4, 768, 2048], P('expert', None, 'dp')
- grad_router: float32 [2048, 4], replicated
The draws below stay inside these ranges and needn't reach their ends.
Inputs may be any that keep to these rules, and one draw needn't show every extreme that they name: `lengths`: every device's block of 2 users holds one user with all 1024 events. `neg_index`: indices of users anywhere in the batch. `routes`: each row names two different experts; among the rows of one device no expert is named more than 128 times, a bound that some block reaches.
All inputs are finite; a program needn't handle non-finite values.
Results may differ from the reference program's by a relative error of at most 0.017.
Values may be sent and summed in bfloat16 or wider, within the bound.
No kernel may reach another device: no remote copies, remote signals or barrier semaphores. Data moves between devices by JAX's collectives and lax.ppermute only.
A program may use at most 128 MiB of HBM per device.

```python
import math
import jax
import jax.numpy as jnp
import numpy as np
from jax import lax

D = 2048
HEADS = 16
HEAD = 128
FF = 768
EXPERTS = 4
CANDS = 64
NEG = 63
U_DEV = 2
HIST = 1024
CAP = 128
USERS = 64
ROWS = 4096
N_DP = 8
N_EXPERT = 4


def draw_lengths(key, part):
    key_len = jax.random.fold_in(key, 11)
    key_full = jax.random.fold_in(key, 12)
    low_bound = max(1, HIST // 16)
    drawn = jax.random.randint(key_len, (USERS,), low_bound, HIST + 1, dtype=jnp.int32)
    device_count = USERS // U_DEV
    chosen = jax.random.randint(key_full, (device_count,), 0, U_DEV, dtype=jnp.int32)
    full_rows = jnp.arange(device_count, dtype=jnp.int32) * U_DEV + chosen
    short_row = (chosen[0] + 1) % U_DEV
    drawn = drawn.at[short_row].set(low_bound)
    return drawn.at[full_rows].set(HIST)


def draw_user_query(key, part):
    base_vals = jax.random.normal(jax.random.fold_in(key, 21), (USERS, D), jnp.float32)
    return jnp.clip(base_vals, -1000.0, 1000.0).astype(jnp.bfloat16)


def place_ends(values, stream_key, smallest, largest):
    index_at = [jax.random.randint(jax.random.fold_in(stream_key, axis), (), 0, length) for axis, length in enumerate(values.shape)]
    longest = values.shape.index(max(values.shape))
    beside = index_at[:longest] + [(index_at[longest] + 1) % values.shape[longest]] + index_at[longest + 1:]
    return values.at[tuple(index_at)].set(smallest).at[tuple(beside)].set(largest)


def shard_levels(rng, shape, shards, least, top_value):
    def one(dim, parts):
        heights = jax.random.uniform(jax.random.fold_in(jax.random.fold_in(rng, 6), dim), (parts,), jnp.float32, least / len(shards), top_value / len(shards))
        return jnp.repeat(jnp.exp(heights), shape[dim] // parts).reshape((-1,) + (1,) * (len(shape) - dim - 1))

    gain = one(*shards[0])
    for cut in shards[1:]:
        gain = gain * one(*cut)
    return gain


def shared_out(key, own, number, rows, count, top, reach, skew):
    order = jax.random.permutation(key, count)
    packed, ordinary = load_shares(count, rows * top, reach, skew, True), load_shares(count, rows * top, reach, skew, False)
    places = jnp.arange(count)

    def named(sizes, offset_by):
        used = int((sizes > 0).sum())
        fixed = max(1, used // 4)
        passed = fixed + (places - fixed + offset_by * (used - fixed)) % max(1, count - fixed)
        return jnp.zeros((count,), jnp.int32).at[order[jnp.where(places < fixed, places, passed)]].set(jnp.asarray(sizes, jnp.int32))

    sizes = jnp.where(number % 4 == 0, named(packed, number // 4), named(ordinary, number - number // 4 - 1))
    mixed = jax.random.permutation(jax.random.fold_in(own, 3), count)
    giver, sink = mixed[0:count // 2 * 2:2], mixed[1:count // 2 * 2:2]
    margin = jnp.minimum(sizes[giver] - 1, reach - sizes[sink]) // 2
    margin = jnp.where((giver == order[0]) | (sink == order[0]) | (sizes[sink] == 0), 0, jnp.maximum(margin, 0))
    passed = jax.random.randint(jax.random.fold_in(own, 4), (count // 2,), 0, 1 << 20) % (margin + 1)
    sizes = sizes.at[giver].add(-passed).at[sink].add(passed)
    labels = jnp.searchsorted(jnp.cumsum(sizes), jnp.arange(rows * top), side="right").astype(jnp.int32)
    listing = labels.reshape(top, rows).T
    listing = listing[jax.random.permutation(jax.random.fold_in(own, 1), rows)]
    offset_by = jax.random.randint(jax.random.fold_in(own, 2), (rows, 1), 0, top)
    return jnp.take_along_axis(listing, (jnp.arange(top)[None, :] + offset_by) % top, axis=1)


def load_shares(amount, total, reach, skew, full):
    portions = [(1 << 20) // math.isqrt(rank ** skew) + 1 for rank in range(1, amount + 1)]
    largest = reach if full else min(reach, max(-(-total // amount), total * portions[0] // sum(portions)))
    least = 1 if total - largest >= amount - 1 else 0
    holding, spare = [largest] + [least] * (amount - 1), total - largest - least * (amount - 1)
    while spare > 0:
        free = [i for i in range(1, amount) if holding[i] < largest] or [i for i in range(1, amount) if holding[i] < reach]
        whole, budget = sum([portions[i] for i in free]), spare
        for i in free:
            more = min(reach - holding[i], max(1, budget * portions[i] // whole), spare)
            holding[i] = holding[i] + more
            spare = spare - more
    return np.array(holding)


def centred(key, extent, spread, limit, cuts=(), kind=jnp.bfloat16):
    values = spread * jax.random.normal(key, extent, jnp.float32)
    if cuts:
        values = values * shard_levels(key, extent, cuts, -0.22, 0.18)
    return jnp.clip(values, -limit, limit).astype(kind)


def setup_inputs(seed: int = 0) -> dict:
    seeds = jax.random.split(jax.random.key(seed), 12)
    history = centred(seeds[0], (USERS, HIST, D), 1.0, 6.0, ((0, 32),))
    lengths = draw_lengths(jax.random.fold_in(seeds[11], 71), 0)
    user_query = draw_user_query(jax.random.fold_in(seeds[11], 71), 0)
    pos_item = centred(seeds[3], (USERS, D), 1.0, 6.0, ((0, 32),))
    neg_index = place_ends(jax.random.randint(seeds[4], (USERS, NEG), 0, USERS), jax.random.fold_in(seeds[4], 1), 0, USERS - 1).astype(jnp.int32)
    routes_keys = jax.random.split(jax.random.fold_in(seeds[5], 1), ROWS // (U_DEV * CANDS))
    routes_turns = jax.random.permutation(jax.random.fold_in(seeds[5], 3), ROWS // (U_DEV * CANDS))
    routes = jax.vmap(lambda own, number: shared_out(jax.random.fold_in(seeds[5], 2), own, number, U_DEV * CANDS, EXPERTS, 2, CAP, 2))(routes_keys, routes_turns).reshape((ROWS, 2))
    w_router = centred(seeds[6], (D, EXPERTS), D ** -0.5, 0.125)
    w_gate = centred(seeds[7], (EXPERTS, D, FF), D ** -0.5, 0.125, ((0, 4), (1, 8)))
    w_up = centred(seeds[8], (EXPERTS, D, FF), D ** -0.5, 0.125, ((0, 4), (1, 8)))
    w_down = centred(seeds[9], (EXPERTS, FF, D), FF ** -0.5, 0.21875, ((0, 4), (2, 8)))
    out_gain = jnp.clip(1.0 + 0.15 * jax.random.normal(seeds[10], (D,), jnp.float32), 0.25, 1.75)
    return {"history": history, "lengths": lengths, "user_query": user_query, "pos_item": pos_item, "neg_index": neg_index, "routes": routes, "w_router": w_router, "w_gate": w_gate, "w_up": w_up, "w_down": w_down, "out_gain": out_gain}


norm_eps = 1e-06
loss_scale = 1024.0

def silu_pair(pre_act):
    sigma_val = jax.nn.sigmoid(pre_act)
    return (pre_act * sigma_val, sigma_val * (1.0 + pre_act * (1.0 - sigma_val)))

def rms_round(values):
    scale_inv = lax.rsqrt(lax.optimization_barrier(jnp.mean(values * values, axis=-1, keepdims=True)) + norm_eps)
    return (values * scale_inv).astype(jnp.bfloat16)

def pool_user(block_args):
    hist_rows, hist_len, query_row = block_args
    keys_f = hist_rows.astype(jnp.float32).reshape(HIST, HEADS, HEAD)
    query_f = query_row.astype(jnp.float32).reshape(HEADS, HEAD)
    scores = jnp.einsum('hd,thd->ht', query_f, keys_f) / math.sqrt(HEAD)
    live_mask = (jnp.arange(HIST, dtype=jnp.int32) < hist_len)[None, :]
    scores = jnp.where(live_mask, scores, -1e+30)
    top_val = lax.optimization_barrier(jnp.max(scores, axis=-1, keepdims=True))
    weights = jnp.where(live_mask, jnp.exp(scores - top_val), 0.0)
    attn_probs = (weights / lax.optimization_barrier(jnp.sum(weights, axis=-1, keepdims=True))).astype(jnp.bfloat16)
    pooled = jnp.einsum('ht,thd->hd', attn_probs.astype(jnp.float32), keys_f)
    return pooled.reshape(D)

def reference(history, lengths, user_query, pos_item, neg_index, routes, w_router, w_gate, w_up, w_down, out_gain):
    context = lax.map(pool_user, (history, lengths, user_query))
    candidates = jnp.concatenate([pos_item[:, None, :], pos_item[neg_index]], axis=1)
    x_sum = candidates.astype(jnp.float32) + context[:, None, :]
    normed = rms_round(x_sum).reshape(ROWS, D)
    logits = jnp.dot(normed, w_router, preferred_element_type=jnp.float32)
    affinity = jax.nn.sigmoid(jnp.take_along_axis(logits, routes, axis=1))
    aff_total = lax.optimization_barrier(jnp.sum(affinity, axis=1, keepdims=True))
    mix = affinity / aff_total
    per_dev = 2 * CANDS * U_DEV
    n_devices = N_DP * N_EXPERT
    slot_count = N_EXPERT * CAP
    flat_routes = routes.reshape(n_devices, per_dev)
    one_hot = (flat_routes[..., None] == jnp.arange(EXPERTS, dtype=jnp.int32)).astype(jnp.int32)
    slot_rank = lax.optimization_barrier(jnp.sum(jnp.cumsum(one_hot, axis=1) * one_hot, axis=-1)) - 1
    device_ids = jnp.arange(n_devices, dtype=jnp.int32)[:, None] + jnp.zeros_like(flat_routes)
    group_ids = device_ids // N_EXPERT
    buffer_pos = device_ids % N_EXPERT * CAP + slot_rank
    assign_ids = jnp.arange(n_devices * per_dev, dtype=jnp.int32).reshape(n_devices, per_dev)
    table = jnp.full((EXPERTS, N_DP, slot_count), -1, jnp.int32)
    table = table.at[flat_routes, group_ids, buffer_pos].set(assign_ids)

    def expert_block(expert_id, slot_ids):
        live_mask = (slot_ids >= 0)[:, None]
        rows_in = jnp.where(live_mask, normed[jnp.maximum(slot_ids, 0) // 2], jnp.zeros((), jnp.bfloat16))
        gate_pre = jnp.dot(rows_in, w_gate[expert_id], preferred_element_type=jnp.float32)
        up_pre = jnp.dot(rows_in, w_up[expert_id], preferred_element_type=jnp.float32)
        silu_val, silu_grad = silu_pair(gate_pre)
        hidden = (silu_val * up_pre).astype(jnp.bfloat16)
        return (live_mask, rows_in, up_pre, silu_val, silu_grad, hidden)

    def forward_block(block_args):
        expert_id, slot_ids = block_args
        hidden = expert_block(expert_id, slot_ids)[5]
        return jnp.dot(hidden, w_down[expert_id], preferred_element_type=jnp.float32).astype(jnp.bfloat16)
    expert_of = jnp.arange(EXPERTS * N_DP, dtype=jnp.int32) // N_DP
    block_outs = lax.map(forward_block, (expert_of, table.reshape(EXPERTS * N_DP, slot_count)))
    expert_out = block_outs[flat_routes * N_DP + group_ids, buffer_pos].reshape(ROWS, 2, D)
    moe_sum = mix[:, 0:1] * expert_out[:, 0].astype(jnp.float32) + mix[:, 1:2] * expert_out[:, 1].astype(jnp.float32)
    h_rows = (x_sum.reshape(ROWS, D) + moe_sum).reshape(USERS, CANDS, D)
    inv_rms = lax.rsqrt(lax.optimization_barrier(jnp.mean(h_rows * h_rows, axis=-1, keepdims=True)) + norm_eps)
    unit_rows = h_rows * inv_rms
    scored = unit_rows * out_gain
    query_f = user_query.astype(jnp.float32)
    listwise = jnp.einsum('ucd,ud->uc', scored, query_f, precision=lax.Precision.HIGHEST) / math.sqrt(D)
    top_val = lax.optimization_barrier(jnp.max(listwise, axis=-1, keepdims=True))
    expo = jnp.exp(listwise - top_val)
    expo_total = lax.optimization_barrier(jnp.sum(expo, axis=-1, keepdims=True))
    losses = jnp.log(expo_total[:, 0]) + top_val[:, 0] - listwise[:, 0]
    first_one = (jnp.arange(CANDS, dtype=jnp.int32) == 0).astype(jnp.float32)[None, :]
    d_list = loss_scale * (expo / expo_total - first_one)
    d_scored = d_list[..., None] * query_f[:, None, :] / math.sqrt(D)
    d_unit = d_scored * out_gain
    d_h = inv_rms * (d_unit - unit_rows * lax.optimization_barrier(jnp.mean(d_unit * unit_rows, axis=-1, keepdims=True)))
    d_h = d_h.reshape(ROWS, D)
    d_out = (mix[:, :, None] * d_h[:, None, :]).astype(jnp.bfloat16)
    d_mix = lax.optimization_barrier(jnp.sum(d_h[:, None, :] * expert_out.astype(jnp.float32), axis=-1))
    mix_dot = lax.optimization_barrier(jnp.sum(mix * d_mix, axis=1, keepdims=True))
    d_aff = (d_mix - mix_dot) / aff_total
    d_pick = d_aff * affinity * (1.0 - affinity)
    route_hot = (routes[:, :, None] == jnp.arange(EXPERTS, dtype=jnp.int32)).astype(jnp.float32)
    d_logits = lax.optimization_barrier(jnp.sum(route_hot * d_pick[:, :, None], axis=1)).astype(jnp.bfloat16)
    grad_router = jnp.dot(normed.T, d_logits, preferred_element_type=jnp.float32)
    d_flat = d_out.reshape(ROWS * 2, D)

    def expert_grads(expert_id):

        def per_group(running, slot_ids):
            live_mask, rows_in, up_pre, silu_val, silu_grad, hidden = expert_block(expert_id, slot_ids)
            grad_rows = jnp.where(live_mask, d_flat[jnp.maximum(slot_ids, 0)], jnp.zeros((), jnp.bfloat16))
            d_hidden = jnp.dot(grad_rows, w_down[expert_id].T, preferred_element_type=jnp.float32)
            d_gate = (d_hidden * up_pre * silu_grad).astype(jnp.bfloat16)
            d_up = (d_hidden * silu_val).astype(jnp.bfloat16)
            part_gate = jnp.dot(rows_in.T, d_gate, preferred_element_type=jnp.float32).astype(jnp.bfloat16)
            part_up = jnp.dot(rows_in.T, d_up, preferred_element_type=jnp.float32).astype(jnp.bfloat16)
            part_down = jnp.dot(hidden.T, grad_rows, preferred_element_type=jnp.float32).astype(jnp.bfloat16)
            part_gate, part_up, part_down = lax.optimization_barrier((part_gate, part_up, part_down))
            return ((running[0] + part_gate.astype(jnp.float32), running[1] + part_up.astype(jnp.float32), running[2] + part_down.astype(jnp.float32)), None)
        init = (jnp.zeros((D, FF), jnp.float32), jnp.zeros((D, FF), jnp.float32), jnp.zeros((FF, D), jnp.float32))
        summed, _ = lax.scan(per_group, init, table[expert_id])
        return summed
    grad_gate, grad_up, grad_down = lax.map(expert_grads, jnp.arange(EXPERTS, dtype=jnp.int32))
    return (losses, grad_gate, grad_up, grad_down, grad_router)
```

```python
import math

import jax
import jax.numpy as jnp
from jax import lax
from jax.sharding import PartitionSpec as P

CANDS = 64
HEAD = 128

norm_eps = 1e-06
loss_scale = 1024.0


def silu_pair(pre_act):
    sigma_val = jax.nn.sigmoid(pre_act)
    return (pre_act * sigma_val, sigma_val * (1.0 + pre_act * (1.0 - sigma_val)))


def rms_round(values):
    scale_inv = lax.rsqrt(jnp.mean(values * values, axis=-1, keepdims=True) + norm_eps)
    return (values * scale_inv).astype(jnp.bfloat16)


def dp_shift(value, step):
    size = lax.axis_size("dp")
    nz = size // 2
    return lax.ppermute(
        value, "dp", [(2 * z + c, 2 * ((z + step) % nz) + c) for z in range(nz) for c in range(2)]
    )


def dp_pairs(value, targets):
    return lax.ppermute(
        value, "dp", [(2 * z + c, 2 * t + c) for z, t in enumerate(targets) for c in range(2)]
    )


def core_swap(value):
    size = lax.axis_size("dp")
    return lax.ppermute(value, "dp", [(i, i ^ 1) for i in range(size)])


def dp_xor(value, mask):
    size = lax.axis_size("dp")
    return lax.ppermute(value, "dp", [(i, i ^ mask) for i in range(size)])


def expert_xor(value, mask):
    size = lax.axis_size("expert")
    return lax.ppermute(value, "expert", [(i, i ^ mask) for i in range(size)])


RELAY_OUT = (2, 0, 3, 1)
RELAY_BACK = (1, 3, 0, 2)


def gather_z(own, z, nz):
    if nz != 4:
        return [own] + [dp_shift(own, j) for j in range(1, nz)]
    below = dp_shift(own, 1)
    above = dp_shift(own, 3)
    relayed = jnp.where(z == 1, above, jnp.where(z == 2, below, own))
    return [own, below, dp_pairs(relayed, RELAY_OUT), above]


def add_round(*terms):
    total = terms[0].astype(jnp.float32)
    for term in terms[1:]:
        total = total + term.astype(jnp.float32)
    return total


def scatter_z(parts, z, nz):
    def pick(step):
        return lax.dynamic_index_in_dim(parts, (z + step) % nz, 0, keepdims=False)

    if nz != 4:
        return add_round(pick(0), *[dp_shift(pick(j), j) for j in range(1, nz)])
    relayed = dp_pairs(pick(2), RELAY_BACK)
    zero = jnp.zeros_like(relayed)
    down = add_round(pick(3), jnp.where(z == 2, relayed, zero)).astype(jnp.bfloat16)
    up = add_round(pick(1), jnp.where(z == 1, relayed, zero)).astype(jnp.bfloat16)
    own = jnp.where((z == 0) | (z == 3), relayed, zero)
    return add_round(pick(0), own, dp_shift(down, 3), dp_shift(up, 1))


def local(
    history,
    lengths,
    user_query,
    pos_item,
    neg_index,
    routes,
    w_router,
    w_gate,
    w_up,
    w_down,
    out_gain,
):
    user_count, hist_len, model_width = history.shape
    head_count = model_width // HEAD
    experts = w_router.shape[1]
    hidden_width = w_gate.shape[2]
    dp_size = lax.axis_size("dp")
    ep_size = lax.axis_size("expert")
    nz = dp_size // 2
    me_dp = lax.axis_index("dp")
    me_ep = lax.axis_index("expert")
    z = me_dp // 2
    core = me_dp % 2
    row_total = user_count * CANDS

    items = jnp.stack([pos_item] + [expert_xor(pos_item, k) for k in range(1, ep_size)])
    items = jnp.stack([items] + [dp_shift(items, j) for j in range(1, nz)])
    items = jnp.stack([items, core_swap(items)]).reshape(-1, model_width)

    def gather_weight(own, axis):
        slots = gather_z(own, z, nz)
        return slots + [core_swap(s) for s in slots]

    def place(slots, axis):
        width = slots[0].shape[axis]
        shape = list(slots[0].shape)
        shape[axis] = width * dp_size
        full = jnp.zeros(shape, slots[0].dtype)
        for i, s in enumerate(slots):
            j, other = i % nz, i // nz
            index = ((z - j) % nz) * 2 + (core ^ other)
            full = lax.dynamic_update_slice_in_dim(full, s, index * width, axis)
        return full

    gate_slots = gather_weight(w_gate[0], 0)
    up_slots = gather_weight(w_up[0], 0)
    down_own, _ = lax.optimization_barrier((w_down[0], (gate_slots[2], up_slots[2])))
    down_slots = gather_weight(down_own, 1)

    query_heads = user_query.reshape(user_count, head_count, HEAD)
    key_heads = history.reshape(user_count, hist_len, head_count, HEAD)
    scores = jnp.einsum(
        "uhd,uthd->uht", query_heads, key_heads, preferred_element_type=jnp.float32
    ) / math.sqrt(HEAD)
    live_mask = jnp.arange(hist_len, dtype=jnp.int32)[None, None, :] < lengths[:, None, None]
    scores = jnp.where(live_mask, scores, -1e30)
    top_val = jnp.max(scores, axis=-1, keepdims=True)
    weights = jnp.where(live_mask, jnp.exp(scores - top_val), 0.0)
    attn_probs = (weights / jnp.sum(weights, axis=-1, keepdims=True)).astype(jnp.bfloat16)
    context = jnp.einsum(
        "uht,uthd->uhd", attn_probs, key_heads, preferred_element_type=jnp.float32
    ).reshape(user_count, model_width)

    owner = neg_index // user_count
    owner_dp, owner_ep = owner // ep_size, owner % ep_size
    slot = (((owner_dp % 2) ^ core) * nz + (z - owner_dp // 2) % nz) * ep_size + (owner_ep ^ me_ep)
    negatives = items[slot * user_count + neg_index % user_count]
    candidates = jnp.concatenate([pos_item[:, None, :], negatives], axis=1)
    x_sum = (candidates.astype(jnp.float32) + context[:, None, :]).reshape(row_total, model_width)
    normed = rms_round(x_sum)
    rows_in = jnp.concatenate([normed] + [expert_xor(normed, k) for k in range(1, ep_size)])

    logits = jnp.dot(normed, w_router, preferred_element_type=jnp.float32)
    route_hot = routes[:, :, None] == jnp.arange(experts, dtype=jnp.int32)
    affinity = jax.nn.sigmoid(jnp.sum(jnp.where(route_hot, logits[:, None, :], 0.0), axis=-1))
    aff_total = jnp.sum(affinity, axis=1, keepdims=True)
    mix = affinity / aff_total
    mix_dense = jnp.sum(jnp.where(route_hot, mix[:, :, None], 0.0), axis=1)
    mix_rows = mix_dense.T
    mix_slots = jnp.stack([mix_rows] + [expert_xor(mix_rows, k) for k in range(1, ep_size)])
    mix_here = lax.dynamic_index_in_dim(mix_slots, me_ep, 1, keepdims=False).reshape(-1, 1)

    gate_full = place(gate_slots, 0)
    up_full = place(up_slots, 0)
    gate_pre = jnp.dot(rows_in, gate_full, preferred_element_type=jnp.float32)
    up_pre = jnp.dot(rows_in, up_full, preferred_element_type=jnp.float32)
    silu_val, silu_grad = silu_pair(gate_pre)
    hidden = (silu_val * up_pre).astype(jnp.bfloat16)
    down_full = place(down_slots, 1)
    expert_out = jnp.dot(hidden, down_full, preferred_element_type=jnp.float32).astype(
        jnp.bfloat16
    )
    expert_out = expert_out.reshape(ep_size, row_total, model_width)
    mixed_in = [expert_out[0]] + [expert_xor(expert_out[k], k) for k in range(1, ep_size)]
    mix_cols = [
        lax.dynamic_index_in_dim(mix_dense, me_ep ^ k, 1, keepdims=True) for k in range(ep_size)
    ]
    h_rows = x_sum
    for col, out in zip(mix_cols, mixed_in):
        h_rows = h_rows + col * out.astype(jnp.float32)
    h_rows = h_rows.reshape(user_count, CANDS, model_width)
    inv_rms = lax.rsqrt(jnp.mean(h_rows * h_rows, axis=-1, keepdims=True) + norm_eps)
    unit_rows = h_rows * inv_rms
    scored = unit_rows * out_gain
    query_f = user_query.astype(jnp.float32)
    listwise = jnp.sum(scored * query_f[:, None, :], axis=-1) / math.sqrt(model_width)
    top_list = jnp.max(listwise, axis=-1, keepdims=True)
    expo = jnp.exp(listwise - top_list)
    expo_total = jnp.sum(expo, axis=-1, keepdims=True)
    losses = jnp.log(expo_total[:, 0]) + top_list[:, 0] - listwise[:, 0]
    first_one = (jnp.arange(CANDS, dtype=jnp.int32) == 0).astype(jnp.float32)[None, :]
    d_list = loss_scale * (expo / expo_total - first_one)
    d_scored = d_list[..., None] * query_f[:, None, :] / math.sqrt(model_width)
    d_unit = d_scored * out_gain
    d_h = inv_rms * (d_unit - unit_rows * jnp.mean(d_unit * unit_rows, axis=-1, keepdims=True))
    d_h = d_h.reshape(row_total, model_width)
    d_send = d_h.astype(jnp.bfloat16)
    d_rows = jnp.concatenate([d_send] + [expert_xor(d_send, k) for k in range(1, ep_size)])

    d_dense = jnp.zeros((row_total, experts), jnp.float32)
    lanes = jnp.arange(experts, dtype=jnp.int32)[None, :]
    for k, out in enumerate(mixed_in):
        dots = jnp.sum(d_h * out.astype(jnp.float32), axis=-1, keepdims=True)
        d_dense = d_dense + jnp.where(lanes == (me_ep ^ k), dots, 0.0)
    mix_dot = jnp.sum(mix_dense * d_dense, axis=1, keepdims=True)
    aff_dense = jnp.sum(jnp.where(route_hot, affinity[:, :, None], 0.0), axis=1)
    d_logits = ((d_dense - mix_dot) / aff_total * aff_dense * (1.0 - aff_dense)).astype(
        jnp.bfloat16
    )
    contract_rows = (((0,), (0,)), ((), ()))
    router_term = lax.dot_general(
        d_logits, normed, contract_rows, preferred_element_type=jnp.float32
    )

    contract_cols = (((1,), (1,)), ((), ()))
    d_hidden = mix_here * lax.dot_general(
        d_rows, down_full, contract_cols, preferred_element_type=jnp.float32
    )
    d_gate = (d_hidden * up_pre * silu_grad).astype(jnp.bfloat16)
    d_up = (d_hidden * silu_val).astype(jnp.bfloat16)
    hidden_mix = (mix_here * hidden.astype(jnp.float32)).astype(jnp.bfloat16)

    def weight_grad(left, right):
        part = lax.dot_general(left, right, contract_rows, preferred_element_type=jnp.float32)
        part = part.astype(jnp.bfloat16).reshape(nz, 2, -1, hidden_width)
        other = lax.dynamic_index_in_dim(part, 1 - core, 1, keepdims=False)
        mine = lax.dynamic_index_in_dim(part, core, 1, keepdims=False)
        both = add_round(mine, core_swap(other)).astype(jnp.bfloat16)
        return scatter_z(both, z, nz)

    grad_down = weight_grad(d_rows, hidden_mix).T[None]
    grad_gate = weight_grad(rows_in, d_gate)[None]
    grad_up = weight_grad(rows_in, d_up)[None]

    mask = 1
    while mask < ep_size:
        router_term = router_term + expert_xor(router_term, mask)
        mask *= 2
    mask = 1
    while mask < dp_size:
        router_term = router_term + dp_xor(router_term, mask)
        mask *= 2
    return (losses, grad_gate, grad_up, grad_down, router_term.T)


def solution(mesh):
    both = ("dp", "expert")
    placed = (
        P(both, None, None),
        P(both),
        P(both, None),
        P(both, None),
        P(both, None),
        P(both, None),
        P(),
        P("expert", "dp", None),
        P("expert", "dp", None),
        P("expert", None, "dp"),
        P(),
    )
    return jax.shard_map(
        local,
        mesh=mesh,
        in_specs=placed,
        out_specs=(
            P(both),
            P("expert", "dp", None),
            P("expert", "dp", None),
            P("expert", None, "dp"),
            P(),
        ),
        check_vma=False,
    )
```

```python
import math

import jax
import jax.numpy as jnp
from jax import lax
from jax.sharding import PartitionSpec as P

CANDS = 64
HEAD = 128

norm_eps = 1e-06
loss_scale = 1024.0


def silu_pair(pre_act):
    sigma_val = jax.nn.sigmoid(pre_act)
    return (pre_act * sigma_val, sigma_val * (1.0 + pre_act * (1.0 - sigma_val)))


def rms_round(values):
    scale_inv = lax.rsqrt(jnp.mean(values * values, axis=-1, keepdims=True) + norm_eps)
    return (values * scale_inv).astype(jnp.bfloat16)


def dp_shift(value, step):
    size = lax.axis_size("dp")
    nz = size // 2
    return lax.ppermute(
        value, "dp", [(2 * z + c, 2 * ((z + step) % nz) + c) for z in range(nz) for c in range(2)]
    )


def dp_pairs(value, targets):
    return lax.ppermute(
        value, "dp", [(2 * z + c, 2 * t + c) for z, t in enumerate(targets) for c in range(2)]
    )


def core_swap(value):
    size = lax.axis_size("dp")
    return lax.ppermute(value, "dp", [(i, i ^ 1) for i in range(size)])


def dp_xor(value, mask):
    size = lax.axis_size("dp")
    return lax.ppermute(value, "dp", [(i, i ^ mask) for i in range(size)])


def expert_xor(value, mask):
    size = lax.axis_size("expert")
    return lax.ppermute(value, "expert", [(i, i ^ mask) for i in range(size)])


RELAY_OUT = (2, 0, 3, 1)
RELAY_BACK = (1, 3, 0, 2)


def column_order(nz):
    return (0, 1, 3, 2) if nz == 4 else tuple(range(nz))


def add_up(*terms):
    total = terms[0].astype(jnp.float32)
    for term in terms[1:]:
        total = total + term.astype(jnp.float32)
    return total


def local(
    history,
    lengths,
    user_query,
    pos_item,
    neg_index,
    routes,
    w_router,
    w_gate,
    w_up,
    w_down,
    out_gain,
):
    user_count, hist_len, model_width = history.shape
    head_count = model_width // HEAD
    experts = w_router.shape[1]
    hidden_width = w_gate.shape[2]
    dp_size = lax.axis_size("dp")
    ep_size = lax.axis_size("expert")
    nz = dp_size // 2
    relay = nz == 4
    me_dp = lax.axis_index("dp")
    me_ep = lax.axis_index("expert")
    z = me_dp // 2
    core = me_dp % 2
    row_total = user_count * CANDS
    slice_width = model_width // dp_size
    order = column_order(nz)
    blocks = [(j, o) for j in order for o in range(2)]
    early = model_width - 2 * slice_width

    def block_index(j, other):
        return ((z - j) % nz) * 2 + (core ^ other)

    def arrange(value, axis):
        return jnp.concatenate(
            [
                lax.dynamic_slice_in_dim(
                    value, block_index(j, o) * slice_width, slice_width, axis
                )
                for j, o in blocks
            ],
            axis=axis,
        )

    def shifts(own):
        with jax.named_scope("wshift"):
            if relay:
                return {0: own, 1: dp_shift(own, 1), 3: dp_shift(own, 3)}
            return {j: dp_shift(own, j) if j else own for j in range(nz)}

    def relays(slots):
        if not relay:
            return slots
        with jax.named_scope("wrelay"):
            payload = jnp.where(z == 1, slots[3], jnp.where(z == 2, slots[1], slots[0]))
            return {**slots, 2: dp_pairs(payload, RELAY_OUT)}

    def swap(value):
        with jax.named_scope("wswap"):
            return core_swap(value)

    with jax.named_scope("items_ep"):
        items = jnp.stack([pos_item] + [expert_xor(pos_item, k) for k in range(1, ep_size)])
    with jax.named_scope("items_z"):
        items = jnp.stack([items] + [dp_shift(items, j) for j in range(1, nz)])
    with jax.named_scope("items_core"):
        items = jnp.stack([items, core_swap(items)]).reshape(-1, model_width)

    gu_own = jnp.concatenate([w_gate[0], w_up[0]], axis=1)
    gu_slots = shifts(gu_own)
    gu_ready = [gu_slots[j] for j in sorted(gu_slots) if j]
    down_own, gu_ready = lax.optimization_barrier((w_down[0], gu_ready))
    for j, value in zip([j for j in sorted(gu_slots) if j], gu_ready):
        gu_slots[j] = value
    gu_slots = relays(gu_slots)
    down_slots = relays(shifts(down_own))

    with jax.named_scope("attention"):
        query_heads = user_query.reshape(user_count, head_count, HEAD)
        key_heads = history.reshape(user_count, hist_len, head_count, HEAD)
        scores = jnp.einsum(
            "uhd,uthd->uht", query_heads, key_heads, preferred_element_type=jnp.float32
        ) / math.sqrt(HEAD)
        live_mask = jnp.arange(hist_len, dtype=jnp.int32)[None, None, :] < lengths[:, None, None]
        scores = jnp.where(live_mask, scores, -1e30)
        top_val = jnp.max(scores, axis=-1, keepdims=True)
        weights = jnp.where(live_mask, jnp.exp(scores - top_val), 0.0)
        attn_probs = (weights / jnp.sum(weights, axis=-1, keepdims=True)).astype(jnp.bfloat16)
        context = jnp.einsum(
            "uht,uthd->uhd", attn_probs, key_heads, preferred_element_type=jnp.float32
        ).reshape(user_count, model_width)

    with jax.named_scope("rows"):
        owner = neg_index // user_count
        owner_dp, owner_ep = owner // ep_size, owner % ep_size
        slot = (((owner_dp % 2) ^ core) * nz + (z - owner_dp // 2) % nz) * ep_size + (
            owner_ep ^ me_ep
        )
        table = arrange(items, 1)
        negatives = table[slot * user_count + neg_index % user_count]
        candidates = jnp.concatenate([table[:user_count, None, :], negatives], axis=1)
        x_sum = candidates.astype(jnp.float32) + arrange(context, 1)[:, None, :]
        x_sum = x_sum.reshape(row_total, model_width)
        normed = rms_round(x_sum)
        gain = arrange(out_gain, 0)
        query_f = arrange(user_query, 1).astype(jnp.float32)
        router = arrange(w_router, 0)
    with jax.named_scope("dispatch"):
        rows_in = jnp.concatenate([normed] + [expert_xor(normed, k) for k in range(1, ep_size)])

    with jax.named_scope("router"):
        logits = jnp.dot(normed, router, preferred_element_type=jnp.float32)
        route_hot = routes[:, :, None] == jnp.arange(experts, dtype=jnp.int32)
        affinity = jax.nn.sigmoid(jnp.sum(jnp.where(route_hot, logits[:, None, :], 0.0), axis=-1))
        aff_total = jnp.sum(affinity, axis=1, keepdims=True)
        mix = affinity / aff_total
        mix_dense = jnp.sum(jnp.where(route_hot, mix[:, :, None], 0.0), axis=1)
        mix_rows = mix_dense.T
        mix_slots = jnp.stack([mix_rows] + [expert_xor(mix_rows, k) for k in range(1, ep_size)])
        mix_here = lax.dynamic_index_in_dim(mix_slots, me_ep, 1, keepdims=False).reshape(-1, 1)
        mix_cols = [
            lax.dynamic_index_in_dim(mix_dense, me_ep ^ k, 1, keepdims=True)
            for k in range(ep_size)
        ]

    def lay(slots, js, axis):
        return jnp.concatenate(
            [part for j in js for part in (slots[j], swap(slots[j]))], axis=axis
        )

    with jax.named_scope("expert_fwd"):
        gu_full = lay(gu_slots, order, 0)
        pre = jnp.dot(rows_in, gu_full, preferred_element_type=jnp.float32)
        gate_pre, up_pre = pre[:, :hidden_width], pre[:, hidden_width:]
        silu_val, silu_grad = silu_pair(gate_pre)
        hidden = (silu_val * up_pre).astype(jnp.bfloat16)

    def returned(columns):
        out = jnp.dot(hidden, columns, preferred_element_type=jnp.float32).astype(jnp.bfloat16)
        out = out.reshape(ep_size, row_total, columns.shape[1])
        return [out[0]] + [expert_xor(out[k], k) for k in range(1, ep_size)]

    with jax.named_scope("return_a"):
        down_a = lay(down_slots, order[:-1], 1)
        out_a = returned(down_a)
    with jax.named_scope("return_b"):
        down_b = lay(down_slots, order[-1:], 1)
        out_b = returned(down_b)
    with jax.named_scope("middle"):
        moe_a, moe_b = x_sum[:, :early], x_sum[:, early:]
        for col, a, b in zip(mix_cols, out_a, out_b):
            moe_a = moe_a + col * a.astype(jnp.float32)
            moe_b = moe_b + col * b.astype(jnp.float32)
        h_rows = jnp.concatenate([moe_a, moe_b], axis=1).reshape(user_count, CANDS, model_width)
        inv_rms = lax.rsqrt(jnp.mean(h_rows * h_rows, axis=-1, keepdims=True) + norm_eps)
        unit_rows = h_rows * inv_rms
        scored = unit_rows * gain
        listwise = jnp.sum(scored * query_f[:, None, :], axis=-1) / math.sqrt(model_width)
        top_list = jnp.max(listwise, axis=-1, keepdims=True)
        expo = jnp.exp(listwise - top_list)
        expo_total = jnp.sum(expo, axis=-1, keepdims=True)
        losses = jnp.log(expo_total[:, 0]) + top_list[:, 0] - listwise[:, 0]
        first_one = (jnp.arange(CANDS, dtype=jnp.int32) == 0).astype(jnp.float32)[None, :]
        d_list = loss_scale * (expo / expo_total - first_one)
        d_scored = d_list[..., None] * query_f[:, None, :] / math.sqrt(model_width)
        d_unit = d_scored * gain
        d_h = inv_rms * (d_unit - unit_rows * jnp.mean(d_unit * unit_rows, axis=-1, keepdims=True))
        d_h = d_h.reshape(row_total, model_width)
        d_send = d_h.astype(jnp.bfloat16)
    with jax.named_scope("dh_b"):
        piece = d_send[:, early:]
        d_b = jnp.concatenate([piece] + [expert_xor(piece, k) for k in range(1, ep_size)])
    with jax.named_scope("dh_a"):
        piece = d_send[:, :early]
        d_a = jnp.concatenate([piece] + [expert_xor(piece, k) for k in range(1, ep_size)])

    contract_rows = (((0,), (0,)), ((), ()))
    contract_cols = (((1,), (1,)), ((), ()))
    hidden_mix = (mix_here * hidden.astype(jnp.float32)).astype(jnp.bfloat16)

    def chip_terms(left, right):
        part = lax.dot_general(left, right, contract_rows, preferred_element_type=jnp.float32)
        part = part.astype(jnp.bfloat16).reshape(-1, 2, slice_width, right.shape[1])
        return add_up(part[:, 0], core_swap(part[:, 1])).astype(jnp.bfloat16)

    def send_relay(term):
        return dp_pairs(term, RELAY_BACK) if relay else None

    def send_rest(terms, last, relayed):
        by_chip = {j: terms[i] for i, j in enumerate(order[:-1])}
        if not relay:
            by_chip[order[-1]] = last
            return add_up(by_chip[0], *[dp_shift(by_chip[j], nz - j) for j in range(1, nz)])
        zero = jnp.zeros_like(relayed)
        down = add_up(by_chip[1], jnp.where(z == 2, relayed, zero)).astype(jnp.bfloat16)
        up = add_up(by_chip[3], jnp.where(z == 1, relayed, zero)).astype(jnp.bfloat16)
        own = jnp.where((z == 0) | (z == 3), relayed, zero)
        return add_up(by_chip[0], own, dp_shift(down, 3), dp_shift(up, 1))

    with jax.named_scope("gdown_b"):
        last_down = chip_terms(d_b, hidden_mix)[0]
        relay_down = send_relay(last_down)
        last_down, d_a = lax.optimization_barrier((last_down, d_a))
    with jax.named_scope("gdown_a"):
        terms_down = chip_terms(d_a, hidden_mix)
        terms_down, d_a = lax.optimization_barrier((terms_down, d_a))
    with jax.named_scope("dhidden"):
        d_hidden = lax.dot_general(
            d_a, down_a, contract_cols, preferred_element_type=jnp.float32
        ) + lax.dot_general(d_b, down_b, contract_cols, preferred_element_type=jnp.float32)
        d_hidden = mix_here * d_hidden
        d_pre = jnp.concatenate(
            [
                (d_hidden * up_pre * silu_grad).astype(jnp.bfloat16),
                (d_hidden * silu_val).astype(jnp.bfloat16),
            ],
            axis=1,
        )
    with jax.named_scope("ggu_b"):
        last_gu = chip_terms(rows_in[:, early:], d_pre)[0]
        relay_gu = send_relay(last_gu)
        last_gu, d_pre = lax.optimization_barrier((last_gu, d_pre))
    with jax.named_scope("gdown_sum"):
        sum_down = send_rest(terms_down, last_down, relay_down)
    with jax.named_scope("ggu_a"):
        terms_gu = chip_terms(rows_in[:, :early], d_pre)
        sum_gu = send_rest(terms_gu, last_gu, relay_gu)

    with jax.named_scope("grouter"):
        d_dense = jnp.zeros((row_total, experts), jnp.float32)
        lanes = jnp.arange(experts, dtype=jnp.int32)[None, :]
        for k, (a, b) in enumerate(zip(out_a, out_b)):
            dots = jnp.sum(d_h[:, :early] * a.astype(jnp.float32), axis=-1, keepdims=True)
            dots += jnp.sum(d_h[:, early:] * b.astype(jnp.float32), axis=-1, keepdims=True)
            d_dense = d_dense + jnp.where(lanes == (me_ep ^ k), dots, 0.0)
        mix_dot = jnp.sum(mix_dense * d_dense, axis=1, keepdims=True)
        aff_dense = jnp.sum(jnp.where(route_hot, affinity[:, :, None], 0.0), axis=1)
        d_logits = ((d_dense - mix_dot) / aff_total * aff_dense * (1.0 - aff_dense)).astype(
            jnp.bfloat16
        )
        arranged = lax.dot_general(
            d_logits, normed, contract_rows, preferred_element_type=jnp.float32
        )
        router_term = jnp.zeros_like(arranged)
        for i, (j, o) in enumerate(blocks):
            router_term = lax.dynamic_update_slice_in_dim(
                router_term,
                arranged[:, i * slice_width : (i + 1) * slice_width],
                block_index(j, o) * slice_width,
                1,
            )
        mask = 1
        while mask < ep_size:
            router_term = router_term + expert_xor(router_term, mask)
            mask *= 2
        mask = 1
        while mask < dp_size:
            router_term = router_term + dp_xor(router_term, mask)
            mask *= 2
    return (
        losses,
        sum_gu[:, :hidden_width][None],
        sum_gu[:, hidden_width:][None],
        sum_down.T[None],
        router_term.T,
    )


def solution(mesh):
    both = ("dp", "expert")
    placed = (
        P(both, None, None),
        P(both),
        P(both, None),
        P(both, None),
        P(both, None),
        P(both, None),
        P(),
        P("expert", "dp", None),
        P("expert", "dp", None),
        P("expert", None, "dp"),
        P(),
    )
    return jax.shard_map(
        local,
        mesh=mesh,
        in_specs=placed,
        out_specs=(
            P(both),
            P("expert", "dp", None),
            P("expert", "dp", None),
            P("expert", None, "dp"),
            P(),
        ),
        check_vma=False,
    )
```

```python
import math

import jax
import jax.numpy as jnp
from jax import lax
from jax.sharding import PartitionSpec as P


CANDS = 64
HEAD = 128

norm_eps = 1e-06
loss_scale = 1024.0


def silu_pair(pre_act):
    sigma_val = jax.nn.sigmoid(pre_act)
    return (pre_act * sigma_val, sigma_val * (1.0 + pre_act * (1.0 - sigma_val)))


def rms_round(values):
    scale_inv = lax.rsqrt(jnp.mean(values * values, axis=-1, keepdims=True) + norm_eps)
    return (values * scale_inv).astype(jnp.bfloat16)


def dp_shift(value, step):
    size = lax.axis_size("dp")
    nz = size // 2
    return lax.ppermute(
        value, "dp", [(2 * z + c, 2 * ((z + step) % nz) + c) for z in range(nz) for c in range(2)]
    )


def dp_pairs(value, targets):
    return lax.ppermute(
        value, "dp", [(2 * z + c, 2 * t + c) for z, t in enumerate(targets) for c in range(2)]
    )


def core_swap(value):
    size = lax.axis_size("dp")
    return lax.ppermute(value, "dp", [(i, i ^ 1) for i in range(size)])


def dp_xor(value, mask):
    size = lax.axis_size("dp")
    return lax.ppermute(value, "dp", [(i, i ^ mask) for i in range(size)])


def expert_xor(value, mask):
    size = lax.axis_size("expert")
    return lax.ppermute(value, "expert", [(i, i ^ mask) for i in range(size)])


RELAY_OUT = (2, 0, 3, 1)
RELAY_BACK = (1, 3, 0, 2)


def column_order(nz):
    return (0, 1, 3, 2) if nz == 4 else tuple(range(nz))


def add_up(*terms):
    total = terms[0].astype(jnp.float32)
    for term in terms[1:]:
        total = total + term.astype(jnp.float32)
    return total


def local(
    history,
    lengths,
    user_query,
    pos_item,
    neg_index,
    routes,
    w_router,
    w_gate,
    w_up,
    w_down,
    out_gain,
):
    user_count, hist_len, model_width = history.shape
    head_count = model_width // HEAD
    experts = w_router.shape[1]
    hidden_width = w_gate.shape[2]
    dp_size = lax.axis_size("dp")
    ep_size = lax.axis_size("expert")
    nz = dp_size // 2
    relay = nz == 4
    me_dp = lax.axis_index("dp")
    me_ep = lax.axis_index("expert")
    z = me_dp // 2
    core = me_dp % 2
    row_total = user_count * CANDS
    slice_width = model_width // dp_size
    order = column_order(nz)
    blocks = [(j, o) for j in order for o in range(2)]
    early = model_width - 2 * slice_width

    def block_index(j, other):
        return ((z - j) % nz) * 2 + (core ^ other)

    def arrange(value, axis):
        return jnp.concatenate(
            [
                lax.dynamic_slice_in_dim(
                    value, block_index(j, o) * slice_width, slice_width, axis
                )
                for j, o in blocks
            ],
            axis=axis,
        )

    def shifts(own):
        if relay:
            return {0: own, 1: dp_shift(own, 1), 3: dp_shift(own, 3)}
        return {j: dp_shift(own, j) if j else own for j in range(nz)}

    def relays(slots):
        if not relay:
            return slots
        payload = jnp.where(z == 1, slots[3], jnp.where(z == 2, slots[1], slots[0]))
        return {**slots, 2: dp_pairs(payload, RELAY_OUT)}

    items = jnp.stack([pos_item] + [expert_xor(pos_item, k) for k in range(1, ep_size)])
    items = jnp.stack([items] + [dp_shift(items, j) for j in range(1, nz)])
    items = jnp.stack([items, core_swap(items)]).reshape(-1, model_width)

    gu_own = jnp.concatenate([w_gate[0], w_up[0]], axis=1)
    gu_slots = relays(shifts(gu_own))
    down_slots = relays(shifts(w_down[0]))

    query_heads = user_query.reshape(user_count, head_count, HEAD)
    key_heads = history.reshape(user_count, hist_len, head_count, HEAD)
    scores = jnp.einsum(
        "uhd,uthd->uht", query_heads, key_heads, preferred_element_type=jnp.float32
    ) / math.sqrt(HEAD)
    live_mask = jnp.arange(hist_len, dtype=jnp.int32)[None, None, :] < lengths[:, None, None]
    scores = jnp.where(live_mask, scores, -1e30)
    top_val = jnp.max(scores, axis=-1, keepdims=True)
    weights = jnp.where(live_mask, jnp.exp(scores - top_val), 0.0)
    attn_probs = (weights / jnp.sum(weights, axis=-1, keepdims=True)).astype(jnp.bfloat16)
    context = jnp.einsum(
        "uht,uthd->uhd", attn_probs, key_heads, preferred_element_type=jnp.float32
    ).reshape(user_count, model_width)

    owner = neg_index // user_count
    owner_dp, owner_ep = owner // ep_size, owner % ep_size
    slot = (((owner_dp % 2) ^ core) * nz + (z - owner_dp // 2) % nz) * ep_size + (owner_ep ^ me_ep)
    table = arrange(items, 1)
    negatives = table[slot * user_count + neg_index % user_count]
    candidates = jnp.concatenate([table[:user_count, None, :], negatives], axis=1)
    x_sum = candidates.astype(jnp.float32) + arrange(context, 1)[:, None, :]
    x_sum = x_sum.reshape(row_total, model_width)
    normed = rms_round(x_sum)
    gain = arrange(out_gain, 0)
    query_f = arrange(user_query, 1).astype(jnp.float32)
    router = arrange(w_router, 0)
    rows_in = jnp.concatenate([normed] + [expert_xor(normed, k) for k in range(1, ep_size)])

    logits = jnp.dot(normed, router, preferred_element_type=jnp.float32)
    route_hot = routes[:, :, None] == jnp.arange(experts, dtype=jnp.int32)
    affinity = jax.nn.sigmoid(jnp.sum(jnp.where(route_hot, logits[:, None, :], 0.0), axis=-1))
    aff_total = jnp.sum(affinity, axis=1, keepdims=True)
    mix = affinity / aff_total
    mix_dense = jnp.sum(jnp.where(route_hot, mix[:, :, None], 0.0), axis=1)
    mix_rows = mix_dense.T
    mix_slots = jnp.stack([mix_rows] + [expert_xor(mix_rows, k) for k in range(1, ep_size)])
    mix_here = lax.dynamic_index_in_dim(mix_slots, me_ep, 1, keepdims=False).reshape(-1, 1)
    mix_cols = [
        lax.dynamic_index_in_dim(mix_dense, me_ep ^ k, 1, keepdims=True)
        for k in range(ep_size)
    ]

    def lay(slots, js, axis):
        return jnp.concatenate(
            [part for j in js for part in (slots[j], core_swap(slots[j]))], axis=axis
        )

    gu_full = lay(gu_slots, order, 0)
    pre = jnp.dot(rows_in, gu_full, preferred_element_type=jnp.float32)
    gate_pre, up_pre = pre[:, :hidden_width], pre[:, hidden_width:]
    silu_val, silu_grad = silu_pair(gate_pre)
    hidden = (silu_val * up_pre).astype(jnp.bfloat16)
    hidden_mix = (mix_here * hidden.astype(jnp.float32)).astype(jnp.bfloat16)
    gate_slope = (mix_here * (up_pre * silu_grad)).astype(jnp.bfloat16)
    up_slope = (mix_here * silu_val).astype(jnp.bfloat16)
    hidden, hidden_mix, gate_slope, up_slope = lax.optimization_barrier(
        (hidden, hidden_mix, gate_slope, up_slope)
    )

    def returned(columns):
        out = jnp.dot(hidden, columns, preferred_element_type=jnp.float32)
        out = out.astype(jnp.bfloat16).reshape(ep_size, row_total, columns.shape[1])
        return [out[0]] + [expert_xor(out[k], k) for k in range(1, ep_size)]

    down_a = lay(down_slots, order[:-1], 1)
    out_a = returned(down_a)
    down_b = lay(down_slots, order[-1:], 1)
    out_b = returned(down_b)
    moe_a, moe_b = x_sum[:, :early], x_sum[:, early:]
    for col, a, b in zip(mix_cols, out_a, out_b):
        moe_a = moe_a + col * a.astype(jnp.float32)
        moe_b = moe_b + col * b.astype(jnp.float32)
    h_rows = jnp.concatenate([moe_a, moe_b], axis=1).reshape(user_count, CANDS, model_width)
    inv_rms = lax.rsqrt(jnp.mean(h_rows * h_rows, axis=-1, keepdims=True) + norm_eps)
    unit_rows = h_rows * inv_rms
    scored = unit_rows * gain
    listwise = jnp.sum(scored * query_f[:, None, :], axis=-1) / math.sqrt(model_width)
    top_list = jnp.max(listwise, axis=-1, keepdims=True)
    expo = jnp.exp(listwise - top_list)
    expo_total = jnp.sum(expo, axis=-1, keepdims=True)
    losses = jnp.log(expo_total[:, 0]) + top_list[:, 0] - listwise[:, 0]
    first_one = (jnp.arange(CANDS, dtype=jnp.int32) == 0).astype(jnp.float32)[None, :]
    d_list = loss_scale * (expo / expo_total - first_one)
    d_scored = d_list[..., None] * query_f[:, None, :] / math.sqrt(model_width)
    d_unit = d_scored * gain
    d_h = inv_rms * (d_unit - unit_rows * jnp.mean(d_unit * unit_rows, axis=-1, keepdims=True))
    d_h = d_h.reshape(row_total, model_width)
    d_send = d_h.astype(jnp.bfloat16)
    piece = d_send[:, early:]
    d_b = jnp.concatenate([piece] + [expert_xor(piece, k) for k in range(1, ep_size)])
    piece = d_send[:, :early]
    d_a = jnp.concatenate([piece] + [expert_xor(piece, k) for k in range(1, ep_size)])

    contract_rows = (((0,), (0,)), ((), ()))
    contract_cols = (((1,), (1,)), ((), ()))

    def chip_terms(left, right):
        part = lax.dot_general(left, right, contract_rows, preferred_element_type=jnp.float32)
        part = part.astype(jnp.bfloat16).reshape(-1, 2, slice_width, right.shape[1])
        return add_up(part[:, 0], core_swap(part[:, 1])).astype(jnp.bfloat16)

    def send_relay(term):
        return dp_pairs(term, RELAY_BACK) if relay else None

    def send_rest(terms, last, relayed):
        by_chip = {j: terms[i] for i, j in enumerate(order[:-1])}
        if not relay:
            by_chip[order[-1]] = last
            moved = [dp_shift(by_chip[j], nz - j) for j in range(1, nz)]
            return add_up(by_chip[0], *moved)
        zero = jnp.zeros_like(relayed)
        down = add_up(by_chip[1], jnp.where(z == 2, relayed, zero)).astype(jnp.bfloat16)
        up = add_up(by_chip[3], jnp.where(z == 1, relayed, zero)).astype(jnp.bfloat16)
        own = jnp.where((z == 0) | (z == 3), relayed, zero)
        moved = dp_shift(down, 3), dp_shift(up, 1)
        return add_up(by_chip[0], own, *moved)

    last_down = chip_terms(d_b, hidden_mix)[0]
    relay_down = send_relay(last_down)
    terms_down = chip_terms(d_a, hidden_mix)
    d_hidden = lax.dot_general(
        d_a, down_a, contract_cols, preferred_element_type=jnp.float32
    ) + lax.dot_general(d_b, down_b, contract_cols, preferred_element_type=jnp.float32)
    d_pre = jnp.concatenate(
        [
            (d_hidden * gate_slope.astype(jnp.float32)).astype(jnp.bfloat16),
            (d_hidden * up_slope.astype(jnp.float32)).astype(jnp.bfloat16),
        ],
        axis=1,
    )
    last_gu = chip_terms(rows_in[:, early:], d_pre)[0]
    relay_gu = send_relay(last_gu)
    sum_down = send_rest(terms_down, last_down, relay_down)
    terms_gu = chip_terms(rows_in[:, :early], d_pre)
    sum_gu = send_rest(terms_gu, last_gu, relay_gu)

    d_dense = jnp.zeros((row_total, experts), jnp.float32)
    lanes = jnp.arange(experts, dtype=jnp.int32)[None, :]
    for k, (a, b) in enumerate(zip(out_a, out_b)):
        dots = jnp.sum(d_h[:, :early] * a.astype(jnp.float32), axis=-1, keepdims=True)
        dots += jnp.sum(d_h[:, early:] * b.astype(jnp.float32), axis=-1, keepdims=True)
        d_dense = d_dense + jnp.where(lanes == (me_ep ^ k), dots, 0.0)
    mix_dot = jnp.sum(mix_dense * d_dense, axis=1, keepdims=True)
    aff_dense = jnp.sum(jnp.where(route_hot, affinity[:, :, None], 0.0), axis=1)
    d_logits = ((d_dense - mix_dot) / aff_total * aff_dense * (1.0 - aff_dense)).astype(
        jnp.bfloat16
    )
    arranged = lax.dot_general(d_logits, normed, contract_rows, preferred_element_type=jnp.float32)
    router_term = jnp.zeros_like(arranged)
    for i, (j, o) in enumerate(blocks):
        router_term = lax.dynamic_update_slice_in_dim(
            router_term,
            arranged[:, i * slice_width : (i + 1) * slice_width],
            block_index(j, o) * slice_width,
            1,
        )
    mask = 1
    while mask < ep_size:
        router_term = router_term + expert_xor(router_term, mask)
        mask *= 2
    mask = 1
    while mask < dp_size:
        router_term = router_term + dp_xor(router_term, mask)
        mask *= 2
    return (
        losses,
        sum_gu[:, :hidden_width][None],
        sum_gu[:, hidden_width:][None],
        sum_down.T[None],
        router_term.T,
    )


def solution(mesh):
    both = ("dp", "expert")
    placed = (
        P(both, None, None),
        P(both),
        P(both, None),
        P(both, None),
        P(both, None),
        P(both, None),
        P(),
        P("expert", "dp", None),
        P("expert", "dp", None),
        P("expert", None, "dp"),
        P(),
    )
    return jax.shard_map(
        local,
        mesh=mesh,
        in_specs=placed,
        out_specs=(
            P(both),
            P("expert", "dp", None),
            P("expert", "dp", None),
            P("expert", None, "dp"),
            P(),
        ),
        check_vma=False,
    )
```

```python
import math

import jax
import jax.numpy as jnp
from jax import lax
from jax.sharding import PartitionSpec as P


CANDS = 64
HEAD = 128

norm_eps = 1e-06
loss_scale = 1024.0


def silu_pair(pre_act):
    sigma_val = jax.nn.sigmoid(pre_act)
    return (pre_act * sigma_val, sigma_val * (1.0 + pre_act * (1.0 - sigma_val)))


def rms_round(values):
    scale_inv = lax.rsqrt(jnp.mean(values * values, axis=-1, keepdims=True) + norm_eps)
    return (values * scale_inv).astype(jnp.bfloat16)


def dp_shift(value, step):
    size = lax.axis_size("dp")
    nz = size // 2
    return lax.ppermute(
        value, "dp", [(2 * z + c, 2 * ((z + step) % nz) + c) for z in range(nz) for c in range(2)]
    )


def dp_pairs(value, targets):
    return lax.ppermute(
        value, "dp", [(2 * z + c, 2 * t + c) for z, t in enumerate(targets) for c in range(2)]
    )


def core_swap(value):
    size = lax.axis_size("dp")
    return lax.ppermute(value, "dp", [(i, i ^ 1) for i in range(size)])


def dp_xor(value, mask):
    size = lax.axis_size("dp")
    return lax.ppermute(value, "dp", [(i, i ^ mask) for i in range(size)])


def expert_xor(value, mask):
    size = lax.axis_size("expert")
    return lax.ppermute(value, "expert", [(i, i ^ mask) for i in range(size)])


RELAY_OUT = (2, 0, 3, 1)
RELAY_BACK = (1, 3, 0, 2)


def column_order(nz):
    return (0, 1, 3, 2) if nz == 4 else tuple(range(nz))


def add_up(*terms):
    total = terms[0].astype(jnp.float32)
    for term in terms[1:]:
        total = total + term.astype(jnp.float32)
    return total


def local(
    history,
    lengths,
    user_query,
    pos_item,
    neg_index,
    routes,
    w_router,
    w_gate,
    w_up,
    w_down,
    out_gain,
):
    user_count, hist_len, model_width = history.shape
    head_count = model_width // HEAD
    experts = w_router.shape[1]
    dp_size = lax.axis_size("dp")
    ep_size = lax.axis_size("expert")
    nz = dp_size // 2
    relay = nz == 4
    me_dp = lax.axis_index("dp")
    me_ep = lax.axis_index("expert")
    z = me_dp // 2
    core = me_dp % 2
    row_total = user_count * CANDS
    slice_width = model_width // dp_size
    order = column_order(nz)
    blocks = [(j, o) for o in range(2) for j in order[:-1]] + [(order[-1], o) for o in range(2)]
    early = model_width - 2 * slice_width
    half = early // 2

    def block_index(j, other):
        return ((z - j) % nz) * 2 + (core ^ other)

    def arrange(value, axis):
        return jnp.concatenate(
            [
                lax.dynamic_slice_in_dim(
                    value, block_index(j, o) * slice_width, slice_width, axis
                )
                for j, o in blocks
            ],
            axis=axis,
        )

    def shifts(own):
        if relay:
            return {0: own, 1: dp_shift(own, 1), 3: dp_shift(own, 3)}
        return {j: dp_shift(own, j) if j else own for j in range(nz)}

    def relays(slots):
        if not relay:
            return slots
        payload = jnp.where(z == 1, slots[3], jnp.where(z == 2, slots[1], slots[0]))
        return {**slots, 2: dp_pairs(payload, RELAY_OUT)}

    items = jnp.stack([pos_item] + [dp_shift(pos_item, j) for j in range(1, nz)])
    items = jnp.stack([items] + [expert_xor(items, k) for k in range(1, ep_size)])
    items = jnp.stack([items, core_swap(items)]).reshape(-1, model_width)

    gate_slots = relays(shifts(w_gate[0]))
    up_slots = relays(shifts(w_up[0]))
    down_slots = relays(shifts(w_down[0]))

    query_heads = user_query.reshape(user_count, head_count, HEAD)
    key_heads = history.reshape(user_count, hist_len, head_count, HEAD)
    scores = jnp.einsum(
        "uhd,uthd->uht", query_heads, key_heads, preferred_element_type=jnp.float32
    ) / math.sqrt(HEAD)
    live_mask = jnp.arange(hist_len, dtype=jnp.int32)[None, None, :] < lengths[:, None, None]
    scores = jnp.where(live_mask, scores, -1e30)
    top_val = jnp.max(scores, axis=-1, keepdims=True)
    weights = jnp.where(live_mask, jnp.exp(scores - top_val), 0.0)
    attn_probs = (weights / jnp.sum(weights, axis=-1, keepdims=True)).astype(jnp.bfloat16)
    context = jnp.einsum(
        "uht,uthd->uhd", attn_probs, key_heads, preferred_element_type=jnp.float32
    ).reshape(user_count, model_width)

    owner = neg_index // user_count
    owner_dp, owner_ep = owner // ep_size, owner % ep_size
    slot = (((owner_dp % 2) ^ core) * ep_size + (owner_ep ^ me_ep)) * nz + (z - owner_dp // 2) % nz
    table = arrange(items, 1)
    negatives = table[slot * user_count + neg_index % user_count]
    candidates = jnp.concatenate([table[:user_count, None, :], negatives], axis=1)
    x_sum = candidates.astype(jnp.float32) + arrange(context, 1)[:, None, :]
    x_sum = x_sum.reshape(row_total, model_width)
    normed = rms_round(x_sum)
    gain = arrange(out_gain, 0)
    query_f = arrange(user_query, 1).astype(jnp.float32)
    router = arrange(w_router, 0)
    rows_in = lax.optimization_barrier(
        jnp.concatenate([normed] + [expert_xor(normed, k) for k in range(1, ep_size)])
    )

    logits = jnp.dot(normed, router, preferred_element_type=jnp.float32)
    route_hot = routes[:, :, None] == jnp.arange(experts, dtype=jnp.int32)
    affinity = jax.nn.sigmoid(jnp.sum(jnp.where(route_hot, logits[:, None, :], 0.0), axis=-1))
    aff_total = jnp.sum(affinity, axis=1, keepdims=True)
    mix = affinity / aff_total
    mix_dense = jnp.sum(jnp.where(route_hot, mix[:, :, None], 0.0), axis=1)
    mix_rows = mix_dense.T
    mix_slots = jnp.stack([mix_rows] + [expert_xor(mix_rows, k) for k in range(1, ep_size)])
    mix_here = lax.dynamic_index_in_dim(mix_slots, me_ep, 1, keepdims=False).reshape(-1, 1)
    mix_cols = [
        lax.dynamic_index_in_dim(mix_dense, me_ep ^ k, 1, keepdims=True)
        for k in range(ep_size)
    ]

    def lay(slots, js, axis):
        return jnp.concatenate([slots[j] for j in js] + [core_swap(slots[j]) for j in js], axis=axis)

    def lay_all(slots):
        return jnp.concatenate([lay(slots, order[:-1], 0), lay(slots, order[-1:], 0)])

    gate_slots[0], up_slots[0], down_slots[0], _ = lax.optimization_barrier(
        (gate_slots[0], up_slots[0], down_slots[0], normed)
    )
    gate_full = lay_all(gate_slots)
    up_full = lay_all(up_slots)
    gate_pre = jnp.dot(rows_in, gate_full, preferred_element_type=jnp.float32)
    up_pre = jnp.dot(rows_in, up_full, preferred_element_type=jnp.float32)
    silu_val, silu_grad = silu_pair(gate_pre)
    hidden = (silu_val * up_pre).astype(jnp.bfloat16)
    hidden_mix = (mix_here * hidden.astype(jnp.float32)).astype(jnp.bfloat16)
    gate_slope = (mix_here * (up_pre * silu_grad)).astype(jnp.bfloat16)
    up_slope = (mix_here * silu_val).astype(jnp.bfloat16)
    hidden, hidden_mix, gate_slope, up_slope = lax.optimization_barrier(
        (hidden, hidden_mix, gate_slope, up_slope)
    )

    def returned(columns):
        out = jnp.dot(hidden, columns, preferred_element_type=jnp.float32)
        out = out.astype(jnp.bfloat16).reshape(ep_size, row_total, columns.shape[1])
        return [out[0]] + [expert_xor(out[k], k) for k in range(1, ep_size)]

    down_a = lay(down_slots, order[:-1], 1)
    out_a = returned(down_a)
    down_b = lay(down_slots, order[-1:], 1)
    out_b = returned(down_b)
    moe_a, moe_b = x_sum[:, :early], x_sum[:, early:]
    for col, a, b in zip(mix_cols, out_a, out_b):
        moe_a = moe_a + col * a.astype(jnp.float32)
        moe_b = moe_b + col * b.astype(jnp.float32)
    h_rows = jnp.concatenate([moe_a, moe_b], axis=1).reshape(user_count, CANDS, model_width)
    inv_rms = lax.rsqrt(jnp.mean(h_rows * h_rows, axis=-1, keepdims=True) + norm_eps)
    unit_rows = h_rows * inv_rms
    scored = unit_rows * gain
    listwise = jnp.sum(scored * query_f[:, None, :], axis=-1) / math.sqrt(model_width)
    top_list = jnp.max(listwise, axis=-1, keepdims=True)
    expo = jnp.exp(listwise - top_list)
    expo_total = jnp.sum(expo, axis=-1, keepdims=True)
    losses = jnp.log(expo_total[:, 0]) + top_list[:, 0] - listwise[:, 0]
    first_one = (jnp.arange(CANDS, dtype=jnp.int32) == 0).astype(jnp.float32)[None, :]
    d_list = loss_scale * (expo / expo_total - first_one)
    d_scored = d_list[..., None] * query_f[:, None, :] / math.sqrt(model_width)
    d_unit = d_scored * gain
    d_h = inv_rms * (d_unit - unit_rows * jnp.mean(d_unit * unit_rows, axis=-1, keepdims=True))
    d_h = d_h.reshape(row_total, model_width)
    d_send = d_h.astype(jnp.bfloat16)
    piece = d_send[:, early:]
    d_b = jnp.concatenate([piece] + [expert_xor(piece, k) for k in range(1, ep_size)])
    piece = d_send[:, :early]
    d_a = jnp.concatenate([piece] + [expert_xor(piece, k) for k in range(1, ep_size)])

    contract_rows = (((0,), (0,)), ((), ()))
    contract_cols = (((1,), (1,)), ((), ()))

    def chip_terms(mine, other, right):
        part = lax.dot_general(other, right, contract_rows, preferred_element_type=jnp.float32)
        got = core_swap(part.astype(jnp.bfloat16))
        part = lax.dot_general(mine, right, contract_rows, preferred_element_type=jnp.float32)
        return (part + got.astype(jnp.float32)).astype(jnp.bfloat16)

    def send_relay(term):
        return dp_pairs(term, RELAY_BACK) if relay else None

    def send_rest(terms, last, relayed):
        by_chip = {
            j: terms[i * slice_width : (i + 1) * slice_width] for i, j in enumerate(order[:-1])
        }
        if not relay:
            by_chip[order[-1]] = last
            moved = [dp_shift(by_chip[j], nz - j) for j in range(1, nz)]
            return lambda: add_up(by_chip[0], *moved)
        zero = jnp.zeros_like(relayed)
        down = add_up(by_chip[1], jnp.where(z == 2, relayed, zero)).astype(jnp.bfloat16)
        up = add_up(by_chip[3], jnp.where(z == 1, relayed, zero)).astype(jnp.bfloat16)
        moved = dp_shift(down, 3), dp_shift(up, 1)
        return lambda: add_up(
            by_chip[0], jnp.where((z == 0) | (z == 3), relayed, zero), *moved
        )

    last_down = chip_terms(d_b[:, :slice_width], d_b[:, slice_width:], hidden_mix)
    relay_down = send_relay(last_down)
    terms_down = chip_terms(d_a[:, :half], d_a[:, half:], hidden_mix)
    sum_down = send_rest(terms_down, last_down, relay_down)
    d_hidden = lax.dot_general(
        d_a, down_a, contract_cols, preferred_element_type=jnp.float32
    ) + lax.dot_general(d_b, down_b, contract_cols, preferred_element_type=jnp.float32)
    d_gate = (d_hidden * gate_slope.astype(jnp.float32)).astype(jnp.bfloat16)
    d_up = (d_hidden * up_slope.astype(jnp.float32)).astype(jnp.bfloat16)
    mine_b = rows_in[:, early : early + slice_width]
    other_b = rows_in[:, early + slice_width :]
    last_gate = chip_terms(mine_b, other_b, d_gate)
    relay_gate = send_relay(last_gate)
    last_up = chip_terms(mine_b, other_b, d_up)
    relay_up = send_relay(last_up)
    terms_gate = chip_terms(rows_in[:, :half], rows_in[:, half:early], d_gate)
    terms_up = chip_terms(rows_in[:, :half], rows_in[:, half:early], d_up)
    sum_gate = send_rest(terms_gate, last_gate, relay_gate)
    sum_up = send_rest(terms_up, last_up, relay_up)
    sum_down = sum_down().T[None]
    sum_gate = sum_gate()[None]
    sum_up = sum_up()[None]

    d_dense = jnp.zeros((row_total, experts), jnp.float32)
    lanes = jnp.arange(experts, dtype=jnp.int32)[None, :]
    for k, (a, b) in enumerate(zip(out_a, out_b)):
        dots = jnp.sum(d_h[:, :early] * a.astype(jnp.float32), axis=-1, keepdims=True)
        dots += jnp.sum(d_h[:, early:] * b.astype(jnp.float32), axis=-1, keepdims=True)
        d_dense = d_dense + jnp.where(lanes == (me_ep ^ k), dots, 0.0)
    mix_dot = jnp.sum(mix_dense * d_dense, axis=1, keepdims=True)
    aff_dense = jnp.sum(jnp.where(route_hot, affinity[:, :, None], 0.0), axis=1)
    d_logits = ((d_dense - mix_dot) / aff_total * aff_dense * (1.0 - aff_dense)).astype(
        jnp.bfloat16
    )
    arranged = lax.dot_general(d_logits, normed, contract_rows, preferred_element_type=jnp.float32)
    router_term = jnp.zeros_like(arranged)
    for i, (j, o) in enumerate(blocks):
        router_term = lax.dynamic_update_slice_in_dim(
            router_term,
            arranged[:, i * slice_width : (i + 1) * slice_width],
            block_index(j, o) * slice_width,
            1,
        )
    router_term = router_term + dp_xor(router_term, 1)
    mask = 2
    while mask < dp_size:
        router_term = router_term + dp_xor(router_term, mask)
        mask *= 2
    mask = 1
    while mask < ep_size:
        router_term = router_term + expert_xor(router_term, mask)
        mask *= 2
    return (
        losses,
        sum_gate,
        sum_up,
        sum_down,
        router_term.T,
    )


def solution(mesh):
    both = ("dp", "expert")
    placed = (
        P(both, None, None),
        P(both),
        P(both, None),
        P(both, None),
        P(both, None),
        P(both, None),
        P(),
        P("expert", "dp", None),
        P("expert", "dp", None),
        P("expert", None, "dp"),
        P(),
    )
    return jax.shard_map(
        local,
        mesh=mesh,
        in_specs=placed,
        out_specs=(
            P(both),
            P("expert", "dp", None),
            P("expert", "dp", None),
            P("expert", None, "dp"),
            P(),
        ),
        check_vma=False,
    )
```

```python
import functools
import math

import jax
import jax.numpy as jnp
from jax import lax
from jax.experimental import pallas as pl
from jax.experimental.pallas import tpu as pltpu
from jax.sharding import PartitionSpec as P


CANDS = 64
HEAD = 128

norm_eps = 1e-06
loss_scale = 1024.0


def silu_pair(pre_act):
    sigma_val = jax.nn.sigmoid(pre_act)
    return (pre_act * sigma_val, sigma_val * (1.0 + pre_act * (1.0 - sigma_val)))


def dp_shift(value, step):
    size = lax.axis_size("dp")
    nz = size // 2
    return lax.ppermute(
        value, "dp", [(2 * z + c, 2 * ((z + step) % nz) + c) for z in range(nz) for c in range(2)]
    )


def dp_pairs(value, targets):
    return lax.ppermute(
        value, "dp", [(2 * z + c, 2 * t + c) for z, t in enumerate(targets) for c in range(2)]
    )


def core_swap(value):
    size = lax.axis_size("dp")
    return lax.ppermute(value, "dp", [(i, i ^ 1) for i in range(size)])


def dp_xor(value, mask):
    size = lax.axis_size("dp")
    return lax.ppermute(value, "dp", [(i, i ^ mask) for i in range(size)])


def expert_xor(value, mask):
    size = lax.axis_size("expert")
    return lax.ppermute(value, "expert", [(i, i ^ mask) for i in range(size)])


def expert_exchange(values):
    got = {0: values[0]}
    for k in sorted(range(1, len(values)), key=lambda k: -bin(k).count("1")):
        got[k] = expert_xor(values[k], k)
    return [got[k] for k in range(len(values))]


RELAY_OUT = (2, 0, 3, 1)
RELAY_BACK = (1, 3, 0, 2)


def slot_order(nz):
    return (0, 1, 3, 2) if nz == 4 else tuple(range(nz))


def add_up(*terms):
    total = terms[0].astype(jnp.float32)
    for term in terms[1:]:
        total = total + term.astype(jnp.float32)
    return total


VMEM = pl.BlockSpec(memory_space=pltpu.VMEM)
SMEM = pl.BlockSpec(memory_space=pltpu.SMEM)


def spans_of(index_ref, width):
    return [
        (pl.ds(i * width, width), pl.ds(pl.multiple_of(index_ref[i] * width, width), width))
        for i in range(index_ref.shape[0])
    ]


def arrange_kernel(width, index_ref, *refs):
    half = len(refs) // 2
    for here, there in spans_of(index_ref, width):
        for source, target in zip(refs[:half], refs[half:]):
            target[:, here] = source[:, there].astype(target.dtype)


def place_kernel(width, index_ref, source, target):
    for here, there in spans_of(index_ref, width):
        target[:, there] = source[:, here]


def rows_kernel(width, index_ref, slot_ref, table_ref, context_ref, x_ref, normed_ref):
    rows, depth = x_ref.shape
    users = context_ref.shape[0]
    slots = lax.broadcasted_iota(jnp.int32, (rows, table_ref.shape[0]), 1)
    chosen = (slots == slot_ref[...]).astype(jnp.float32).astype(jnp.bfloat16)
    squares = jnp.zeros((rows, 1), jnp.float32)
    for here, there in spans_of(index_ref, width):
        item = jnp.dot(chosen, table_ref[:, there], preferred_element_type=jnp.float32)
        context = context_ref[:, there]
        shared = jnp.concatenate(
            [jnp.broadcast_to(context[u : u + 1], (rows // users, width)) for u in range(users)]
        )
        value = item + shared
        x_ref[:, here] = value
        squares = squares + jnp.sum(value * value, axis=1, keepdims=True)
    scale = lax.rsqrt(squares / depth + norm_eps)
    for here, _ in spans_of(index_ref, width):
        normed_ref[:, here] = (x_ref[:, here] * scale).astype(jnp.bfloat16)


def like(*pairs):
    return [jax.ShapeDtypeStruct(shape, dtype) for shape, dtype in pairs]


def local(
    history,
    lengths,
    user_query,
    pos_item,
    neg_index,
    routes,
    w_router,
    w_gate,
    w_up,
    w_down,
    out_gain,
):
    user_count, hist_len, model_width = history.shape
    head_count = model_width // HEAD
    experts = w_router.shape[1]
    dp_size = lax.axis_size("dp")
    ep_size = lax.axis_size("expert")
    nz = dp_size // 2
    relay = nz == 4
    me_dp = lax.axis_index("dp")
    me_ep = lax.axis_index("expert")
    z = me_dp // 2
    core = me_dp % 2
    row_total = user_count * CANDS
    slice_width = model_width // dp_size
    order = slot_order(nz)
    last = order[-1]
    blocks = [(j, o) for j in order for o in range(2)]
    spans = {
        j: slice(2 * i * slice_width, 2 * (i + 1) * slice_width) for i, j in enumerate(order)
    }

    block_ids = ((z - jnp.array([j for j, _ in blocks], jnp.int32)) % nz) * 2 + (
        core ^ jnp.array([o for _, o in blocks], jnp.int32)
    )

    def shifts(own):
        if relay:
            return {0: own, 1: dp_shift(own, 1), 3: dp_shift(own, 3)}
        return {j: dp_shift(own, j) if j else own for j in range(nz)}

    def relays(slots):
        if not relay:
            return slots
        payload = jnp.where(z == 1, slots[3], jnp.where(z == 2, slots[1], slots[0]))
        return {**slots, 2: dp_pairs(payload, RELAY_OUT)}

    items = jnp.stack(expert_exchange([pos_item] * ep_size))
    items = jnp.stack([items] + [dp_shift(items, j) for j in range(1, nz)])
    items = jnp.stack([items, core_swap(items)]).reshape(-1, model_width)

    gate_slots = relays(shifts(w_gate[0]))
    up_slots = relays(shifts(w_up[0]))
    down_slots = relays(shifts(w_down[0]))

    query_heads = user_query.reshape(user_count, head_count, HEAD)
    key_heads = history.reshape(user_count, hist_len, head_count, HEAD)
    scores = jnp.einsum(
        "uhd,uthd->uht", query_heads, key_heads, preferred_element_type=jnp.float32
    ) / math.sqrt(HEAD)
    live_mask = jnp.arange(hist_len, dtype=jnp.int32)[None, None, :] < lengths[:, None, None]
    scores = jnp.where(live_mask, scores, -1e30)
    top_val = jnp.max(scores, axis=-1, keepdims=True)
    weights = jnp.where(live_mask, jnp.exp(scores - top_val), 0.0)
    attn_probs = (weights / jnp.sum(weights, axis=-1, keepdims=True)).astype(jnp.bfloat16)
    context = jnp.einsum(
        "uht,uthd->uhd", attn_probs, key_heads, preferred_element_type=jnp.float32
    ).reshape(user_count, model_width)

    query_f, gain, router = pl.pallas_call(
        functools.partial(arrange_kernel, slice_width),
        out_shape=like(
            (user_query.shape, jnp.float32),
            ((1, model_width), jnp.float32),
            ((experts, model_width), jnp.bfloat16),
        ),
        in_specs=[SMEM, VMEM, VMEM, VMEM],
        out_specs=[VMEM] * 3,
        compiler_params=pltpu.CompilerParams(vmem_limit_bytes=2 << 20),
    )(block_ids, user_query, out_gain[None], w_router.T)
    owner = neg_index // user_count
    owner_dp, owner_ep = owner // ep_size, owner % ep_size
    slot = (((owner_dp % 2) ^ core) * nz + (z - owner_dp // 2) % nz) * ep_size + (owner_ep ^ me_ep)
    slot = slot * user_count + neg_index % user_count
    mine = jnp.arange(user_count, dtype=jnp.int32)[:, None]
    slot = jnp.concatenate([mine, slot], axis=1).reshape(row_total, 1)
    x_sum, normed = pl.pallas_call(
        functools.partial(rows_kernel, slice_width),
        out_shape=like(
            ((row_total, model_width), jnp.float32),
            ((row_total, model_width), jnp.bfloat16),
        ),
        in_specs=[SMEM, VMEM, VMEM, VMEM],
        out_specs=[VMEM] * 2,
        compiler_params=pltpu.CompilerParams(vmem_limit_bytes=8 << 20),
    )(block_ids, slot, items, context)
    rows_in = lax.optimization_barrier(
        jnp.concatenate(expert_exchange([normed] * ep_size))
    )

    logits = lax.dot_general(
        normed, router, (((1,), (1,)), ((), ())), preferred_element_type=jnp.float32
    )
    route_hot = routes[:, :, None] == jnp.arange(experts, dtype=jnp.int32)
    affinity = jax.nn.sigmoid(jnp.sum(jnp.where(route_hot, logits[:, None, :], 0.0), axis=-1))
    aff_total = jnp.sum(affinity, axis=1, keepdims=True)
    mix = affinity / aff_total
    mix_dense = jnp.sum(jnp.where(route_hot, mix[:, :, None], 0.0), axis=1)
    mix_rows = mix_dense.T
    mix_slots = jnp.stack(expert_exchange([mix_rows] * ep_size))
    mix_here = lax.dynamic_index_in_dim(mix_slots, me_ep, 1, keepdims=False).reshape(-1, 1)
    mix_cols = [
        lax.dynamic_index_in_dim(mix_dense, me_ep ^ k, 1, keepdims=True)
        for k in range(ep_size)
    ]

    def lay(slots, j, axis):
        return jnp.concatenate([slots[j], core_swap(slots[j])], axis=axis)

    def lay_all(slots):
        return jnp.concatenate([lay(slots, j, 0) for j in order])

    for slots in (gate_slots, up_slots):
        for j in order[:-1]:
            slots[j], _ = lax.optimization_barrier((slots[j], logits))
    for j in order[:-1]:
        down_slots[j], _ = lax.optimization_barrier((down_slots[j], logits))
    gate_full = lay_all(gate_slots)
    up_full = lay_all(up_slots)
    gate_pre = jnp.dot(rows_in, gate_full, preferred_element_type=jnp.float32)
    up_pre = jnp.dot(rows_in, up_full, preferred_element_type=jnp.float32)
    silu_val, silu_grad = silu_pair(gate_pre)
    hidden = (silu_val * up_pre).astype(jnp.bfloat16)
    hidden_mix = (mix_here * hidden.astype(jnp.float32)).astype(jnp.bfloat16)
    gate_slope = (mix_here * (up_pre * silu_grad)).astype(jnp.bfloat16)
    up_slope = (mix_here * silu_val).astype(jnp.bfloat16)
    hidden, hidden_mix, gate_slope, up_slope = lax.optimization_barrier(
        (hidden, hidden_mix, gate_slope, up_slope)
    )

    def returned(columns):
        out = jnp.dot(hidden, columns, preferred_element_type=jnp.float32)
        out = out.astype(jnp.bfloat16).reshape(ep_size, row_total, columns.shape[1])
        return expert_exchange(list(out))

    downs, outs = {}, {}
    for j in order:
        downs[j] = lay(down_slots, j, 1)
        if relay:
            outs[j] = returned(downs[j])
    if not relay:
        full = jnp.concatenate([downs[j] for j in order], axis=1)
        parts = returned(full)
        outs = {j: [part[:, spans[j]] for part in parts] for j in order}
    moe = []
    for j in order:
        term = x_sum[:, spans[j]]
        for col, part in zip(mix_cols, outs[j]):
            term = term + col * part.astype(jnp.float32)
        moe.append(term)
    h_rows = jnp.concatenate(moe, axis=1).reshape(user_count, CANDS, model_width)
    inv_rms = lax.rsqrt(jnp.mean(h_rows * h_rows, axis=-1, keepdims=True) + norm_eps)
    unit_rows = h_rows * inv_rms
    scored = unit_rows * gain
    listwise = jnp.sum(scored * query_f[:, None, :], axis=-1) / math.sqrt(model_width)
    top_list = jnp.max(listwise, axis=-1, keepdims=True)
    expo = jnp.exp(listwise - top_list)
    expo_total = jnp.sum(expo, axis=-1, keepdims=True)
    losses = jnp.log(expo_total[:, 0]) + top_list[:, 0] - listwise[:, 0]
    first_one = (jnp.arange(CANDS, dtype=jnp.int32) == 0).astype(jnp.float32)[None, :]
    d_list = loss_scale * (expo / expo_total - first_one)
    d_scored = d_list[..., None] * query_f[:, None, :] / math.sqrt(model_width)
    d_unit = d_scored * gain
    d_h = inv_rms * (d_unit - unit_rows * jnp.mean(d_unit * unit_rows, axis=-1, keepdims=True))
    d_h = d_h.reshape(row_total, model_width)
    d_send = d_h.astype(jnp.bfloat16)
    d_parts = {}
    if relay:
        for j in order:
            piece = d_send[:, spans[j]]
            d_parts[j] = jnp.concatenate(expert_exchange([piece] * ep_size))
    else:
        full = jnp.concatenate(expert_exchange([d_send] * ep_size))
        d_parts = {j: full[:, spans[j]] for j in order}

    contract_rows = (((0,), (0,)), ((), ()))
    contract_cols = (((1,), (1,)), ((), ()))

    def chip_terms(left, right):
        half = left.shape[1] // 2
        mine, other = left[:, :half], left[:, half:]
        part = lax.dot_general(other, right, contract_rows, preferred_element_type=jnp.float32)
        got = core_swap(part.astype(jnp.bfloat16))
        part = lax.dot_general(mine, right, contract_rows, preferred_element_type=jnp.float32)
        return (part + got.astype(jnp.float32)).astype(jnp.bfloat16)

    def send_relay(term):
        return dp_pairs(term, RELAY_BACK) if relay else None

    def send_rest(terms, own, relayed):
        if not relay:
            moved = [dp_shift(terms[j], nz - j) for j in range(1, nz)]
            return add_up(own(), *moved)
        zero = jnp.zeros_like(relayed)
        down = add_up(terms[1], jnp.where(z == 2, relayed, zero)).astype(jnp.bfloat16)
        up = add_up(terms[3], jnp.where(z == 1, relayed, zero)).astype(jnp.bfloat16)
        moved = dp_shift(down, 3), dp_shift(up, 1)
        base = lax.optimization_barrier(
            add_up(own(), jnp.where((z == 0) | (z == 3), relayed, zero))
        )
        return add_up(base, *moved)

    row_parts = {j: rows_in[:, spans[j]] for j in order}
    sent = order[:0:-1]
    down_terms = {}
    for j in sent:
        down_terms[j] = chip_terms(d_parts[j], hidden_mix)
    relay_down = send_relay(down_terms[last])
    sum_down = send_rest(down_terms, lambda: chip_terms(d_parts[0], hidden_mix), relay_down)
    d_hidden = sum(
        lax.dot_general(d_parts[j], downs[j], contract_cols, preferred_element_type=jnp.float32)
        for j in order[::-1]
    )
    d_gate = (d_hidden * gate_slope.astype(jnp.float32)).astype(jnp.bfloat16)
    d_up = (d_hidden * up_slope.astype(jnp.float32)).astype(jnp.bfloat16)
    gate_terms, up_terms = {}, {}
    for j in sent:
        gate_terms[j] = chip_terms(row_parts[j], d_gate)
        up_terms[j] = chip_terms(row_parts[j], d_up)
    relay_gate = send_relay(gate_terms[last])
    relay_up = send_relay(up_terms[last])
    sum_gate = send_rest(gate_terms, lambda: chip_terms(row_parts[0], d_gate), relay_gate)
    sum_up = send_rest(up_terms, lambda: chip_terms(row_parts[0], d_up), relay_up)
    sum_down = sum_down.T[None]
    sum_gate = sum_gate[None]
    sum_up = sum_up[None]

    d_dense = jnp.zeros((row_total, experts), jnp.float32)
    lanes = jnp.arange(experts, dtype=jnp.int32)[None, :]
    for k in range(ep_size):
        dots = sum(
            jnp.sum(d_h[:, spans[j]] * outs[j][k].astype(jnp.float32), axis=-1, keepdims=True)
            for j in order
        )
        d_dense = d_dense + jnp.where(lanes == (me_ep ^ k), dots, 0.0)
    mix_dot = jnp.sum(mix_dense * d_dense, axis=1, keepdims=True)
    aff_dense = jnp.sum(jnp.where(route_hot, affinity[:, :, None], 0.0), axis=1)
    d_logits = ((d_dense - mix_dot) / aff_total * aff_dense * (1.0 - aff_dense)).astype(
        jnp.bfloat16
    )
    arranged = lax.dot_general(d_logits, normed, contract_rows, preferred_element_type=jnp.float32)
    router_term = pl.pallas_call(
        functools.partial(place_kernel, slice_width),
        out_shape=jax.ShapeDtypeStruct(arranged.shape, jnp.float32),
        in_specs=[SMEM, VMEM],
        out_specs=VMEM,
        compiler_params=pltpu.CompilerParams(vmem_limit_bytes=2 << 20),
    )(block_ids, arranged)
    router_term = router_term + dp_xor(router_term, 1)
    router_term = router_term + dp_xor(router_term, 2)
    mask = 4
    while mask < dp_size:
        router_term = router_term + dp_xor(router_term, mask)
        mask *= 2
    mask = 1
    while mask < ep_size:
        router_term = router_term + expert_xor(router_term, mask)
        mask *= 2
    grad_router = router_term.T
    return (
        losses,
        sum_gate,
        sum_up,
        sum_down,
        grad_router,
    )


def solution(mesh):
    both = ("dp", "expert")
    placed = (
        P(both, None, None),
        P(both),
        P(both, None),
        P(both, None),
        P(both, None),
        P(both, None),
        P(),
        P("expert", "dp", None),
        P("expert", "dp", None),
        P("expert", None, "dp"),
        P(),
    )
    return jax.shard_map(
        local,
        mesh=mesh,
        in_specs=placed,
        out_specs=(
            P(both),
            P("expert", "dp", None),
            P("expert", "dp", None),
            P("expert", None, "dp"),
            P(),
        ),
        check_vma=False,
    )
```
